256 devices in a mesh: row: 16 (over z, core), col: 4 (over x), depth: 4 (over y).
Axes of the slice: x: 4, y: 4, z: 8, core: 2. Of those that a mesh axis runs over, the one named last changes fastest.
Arguments:
- residual: float32 [2048, 4096], P(('row', 'depth'), 'col'), may hold values from -4 to 4
- amplitudes: float32 [2048, 65536], P('col', ('row', 'depth')), may hold values from -6 to 6
- integrals: float32 [65536, 4096], P(('row', 'depth'), 'col'), may hold values from -0.0390625 to 0.0390625
- t2_mask: int32 [16, 512], P('col', ('row', 'depth')), may hold values from 0 to 1, as said below
- v_mask: int32 [512, 32], P(('row', 'depth'), 'col'), may hold values from 0 to 1, as said below
Outputs:
- updated: float32 [2048, 4096], P(('row', 'depth'), 'col')
The draws below stay inside these ranges and needn't reach their ends.
Inputs may be any that keep to these rules, and one draw needn't show every extreme that they name: `t2_mask`: each entry flags one 128 x 128 amplitude tile as kept (1) or zero (0). `v_mask`: each entry flags one 128 x 128 integral tile as kept (1) or zero (0).
All inputs are finite; a program needn't handle non-finite values.
Results may differ from the reference program's by a relative error of at most 0.0001.
Values sent between devices are 32-bit elements; how exact they have to be, the bound alone decides.
A program may use at most 64 MiB of HBM per device.

```python
import jax
import jax.numpy as jnp
from jax import lax

TILE = 128
NAB = 4096
CD_DEV = 1024
NIJ = 2048
NCD = 65536
IJ_TILES = 16
CD_TILES = 512
AB_TILES = 32


def tile_flags_draw(key, shape, cd_axis):
    counts = jax.random.randint(key, shape, 0, 100)
    position = lax.broadcasted_iota(jnp.int32, shape, cd_axis)
    limit = 15 + 50 * position // CD_TILES
    return (counts < limit).astype(jnp.int32)


def draw_t2_mask(key, part):
    return tile_flags_draw(jax.random.fold_in(key, 11), (IJ_TILES, CD_TILES), 1)


def draw_v_mask(key, part):
    return tile_flags_draw(jax.random.fold_in(key, 23), (CD_TILES, AB_TILES), 0)


def shard_levels(rng, shape, split, low, largest):
    gain = 1.0
    for dim, shards_of in split:
        steps = jax.random.uniform(jax.random.fold_in(jax.random.fold_in(rng, 6), dim), (shards_of,), jnp.float32, low / len(split), largest / len(split))
        gain = gain * jnp.repeat(jnp.exp(steps), shape[dim] // shards_of).reshape((-1,) + (1,) * (len(shape) - 1 - dim))
    return gain


def gaussian(key, extent, scale, reach, pieces=(), held_as=jnp.bfloat16):
    drawn = jax.random.normal(key, extent, jnp.float32) * scale
    if len(pieces) > 0:
        drawn = shard_levels(key, extent, pieces, -0.22, 0.18) * drawn
    return jnp.clip(drawn, min=-reach, max=reach).astype(held_as)


def setup_inputs(seed: int = 0) -> dict:
    key_list = jax.random.split(jax.random.key(seed), 6)
    residual = gaussian(key_list[0], (NIJ, NAB), 0.5, 4.0, ((0, 64), (1, 4)), jnp.float32)
    amplitudes = gaussian(key_list[1], (NIJ, NCD), 1.0, 6.0, ((0, 4), (1, 64)), jnp.float32)
    integrals = gaussian(key_list[2], (NCD, NAB), (2 * NCD // 5) ** -0.5, 0.0390625, ((0, 64), (1, 4)), jnp.float32)
    t2_mask = draw_t2_mask(jax.random.fold_in(key_list[5], 71), 0)
    v_mask = draw_v_mask(jax.random.fold_in(key_list[5], 71), 0)
    return {"residual": residual, "amplitudes": amplitudes, "integrals": integrals, "t2_mask": t2_mask, "v_mask": v_mask}


def apply_flags(matrix, tile_flags):
    tile_rows, tile_cols = tile_flags.shape
    tiled = matrix.reshape(tile_rows, TILE, tile_cols, TILE) * tile_flags.astype(jnp.float32)[:, None, :, None]
    return tiled.reshape(matrix.shape)


def reference(residual, amplitudes, integrals, t2_mask, v_mask):
    per_slab = CD_DEV // TILE

    def add_slab(slab_num, summed):
        first_col = (slab_num * CD_DEV).astype(jnp.int32)
        first_tile = (slab_num * per_slab).astype(jnp.int32)
        amp_slab = lax.dynamic_slice_in_dim(amplitudes, first_col, CD_DEV, 1)
        amp_flags = lax.dynamic_slice_in_dim(t2_mask, first_tile, per_slab, 1)
        int_slab = lax.dynamic_slice_in_dim(integrals, first_col, CD_DEV, 0)
        int_flags = lax.dynamic_slice_in_dim(v_mask, first_tile, per_slab, 0)
        left_side = apply_flags(amp_slab, amp_flags)
        right_side = apply_flags(int_slab, int_flags)
        return summed + jnp.dot(left_side, right_side, precision=lax.Precision.HIGHEST, preferred_element_type=jnp.float32)

    summed = lax.fori_loop(0, NCD // CD_DEV, add_slab, jnp.zeros((NIJ, NAB), jnp.float32))
    return residual + summed
```

```python
import jax
import jax.numpy as jnp
from jax import lax
from jax.experimental import pallas as pl
from jax.experimental.pallas import tpu as pltpu
from jax.sharding import PartitionSpec as P

TILE = 128
NX, NY, NZ = 4, 4, 8
SUB = 8
NH = 32 // SUB
STEPS = 4 * NH
CD = 1024
AB = 1024
HALF = AB // 2
MESH = pl.DeviceIdType.MESH


def expand_lanes(flags):
    values = flags.astype(jnp.float32)
    return jnp.concatenate(
        [jnp.broadcast_to(values[:, q : q + 1], (values.shape[0], TILE)) for q in range(8)],
        axis=1,
    )


def kernel(
    amp, integ, t2_mask, v_mask, out,
    a_all, v_f32, v_hi, v_lo, a_hl, part, c_in, s_sum, y1_in, y2_out, y2_in, r_out, r_own, z_in,
    t2_all, v_flags, a_flags,
    a_send, a_recv, own_sem, v_sem, m_send, m_recv, m_sem,
    c_send, c_recv, y1_send, y1_recv, y2_send, y2_recv, z_send, z_recv,
):
    row = lax.axis_index("row")
    x = lax.axis_index("col")
    y = lax.axis_index("depth")
    z = row // 2
    core = row % 2
    right, left = (x + 1) % NX, (x + 3) % NX
    up, down, far = (y + 1) % NY, (y + 3) % NY, (y + 2) % NY
    sibling = z * 2 + 1 - core

    def own_copy(h, zz):
        return pltpu.make_async_copy(
            amp.at[zz, :, :, pl.ds(h * SUB, SUB), :], a_all.at[h, zz], own_sem.at[h, zz]
        )

    def v_copy(q):
        block = pl.ds(q * TILE, TILE)
        return pltpu.make_async_copy(integ.at[block, :], v_f32.at[block, :], v_sem.at[q])

    m_copy = pltpu.make_async_copy(t2_mask, t2_all.at[x], m_sem.at[0])
    vm_copy = pltpu.make_async_copy(v_mask, v_flags, m_sem.at[1])
    m_copy.start()
    vm_copy.start()
    for q in range(8):
        v_copy(q).start()
    for h in range(NH):
        own_copy(h, 0).start()
        own_copy(h, 1).start()

    barrier = pltpu.get_barrier_semaphore()

    def greet(r, c, d):
        pl.semaphore_signal(barrier, inc=1, device_id=(r, c, d), device_id_type=MESH)

    for k in range(1, NX):
        greet(row, (x + k) % NX, y)
    greet(sibling, x, y)
    greet(row, x, up)
    greet(row, x, down)
    for k in range(1, NZ):
        greet(((z + k) % NZ) * 2 + core, x, y)
    pl.semaphore_wait(barrier, NX - 1 + 3 + NZ - 1)

    def a_own_send(j, side):
        zz = (side + j // NH) % 2
        return pltpu.make_async_remote_copy(
            src_ref=amp.at[zz, :, :, pl.ds((j % NH) * SUB, SUB), :],
            dst_ref=a_all.at[NH + j, side],
            send_sem=a_send.at[side, j],
            recv_sem=a_recv.at[side, j],
            device_id=(row, right if side == 0 else left, y),
            device_id_type=MESH,
        )

    def a_forward(j, side):
        return pltpu.make_async_remote_copy(
            src_ref=a_all.at[NH + j, side],
            dst_ref=a_all.at[3 * NH + j, side],
            send_sem=a_send.at[side, 2 * NH + j],
            recv_sem=a_recv.at[side, 2 * NH + j],
            device_id=(row, right if side == 0 else left, y),
            device_id_type=MESH,
        )

    def flag_send(k):
        return pltpu.make_async_remote_copy(
            src_ref=t2_mask,
            dst_ref=t2_all.at[x],
            send_sem=m_send.at[k - 1],
            recv_sem=m_recv.at[k - 1],
            device_id=(row, (x + k) % NX, y),
            device_id_type=MESH,
        )

    for k in range(1, NX):
        flag_send(k).start()
    for j in range(2 * NH):
        a_own_send(j, 0).start()
        a_own_send(j, 1).start()

    vm_copy.wait()
    flags_v = expand_lanes(v_flags[...])
    for q in range(8):
        v_copy(q).wait()
        rows = slice(q * TILE, (q + 1) * TILE)
        kept = v_f32[rows, :] * flags_v[q : q + 1, :]
        hi = kept.astype(jnp.bfloat16)
        v_hi[rows, :] = hi
        v_lo[rows, :] = (kept - hi.astype(jnp.float32)).astype(jnp.bfloat16)

    m_copy.wait()
    for k in range(1, NX):
        flag_send(k).wait()
    for s in range(NX):
        wide = expand_lanes(t2_all[s])
        for p in range(4):
            a_flags[s * 4 + p] = wide[p : p + 1, :]

    def piece(i, side):
        group = i // NH
        away = (group + 1) // 2
        late = (group // 2) * (1 - group % 2)
        if side == 0:
            return (x + NX - away) % NX, late
        return (x + away) % NX, 1 - late

    def c_copy(i):
        return pltpu.make_async_remote_copy(
            src_ref=part.at[i, :, 1 - core],
            dst_ref=c_in.at[i],
            send_sem=c_send.at[i],
            recv_sem=c_recv.at[i],
            device_id=(sibling, x, y),
            device_id_type=MESH,
        )

    def y1_copy(i, side):
        return pltpu.make_async_remote_copy(
            src_ref=s_sum.at[i, :, far, :, pl.ds(side * HALF, HALF)],
            dst_ref=y1_in.at[i, side],
            send_sem=y1_send.at[side, i],
            recv_sem=y1_recv.at[side, i],
            device_id=(row, x, up if side == 0 else down),
            device_id_type=MESH,
        )

    def y2_copy(i, side):
        return pltpu.make_async_remote_copy(
            src_ref=y2_out.at[i, side],
            dst_ref=y2_in.at[i, side],
            send_sem=y2_send.at[side, i],
            recv_sem=y2_recv.at[side, i],
            device_id=(row, x, up if side == 0 else down),
            device_id_type=MESH,
        )

    def z_copy(i, side, target):
        return pltpu.make_async_remote_copy(
            src_ref=r_out.at[i, side],
            dst_ref=z_in.at[i % NH, (z + NZ - target + NZ - 1) % NZ],
            send_sem=z_send.at[side, i],
            recv_sem=z_recv.at[i % NH],
            device_id=(target * 2 + core, x, y),
            device_id_type=MESH,
        )

    def stage_y1(i):
        c_copy(i).wait_recv()
        for side in range(2):
            s_sum[i, side] = part[i, side, core] + c_in[i, side]
        y1_copy(i, 0).start()
        y1_copy(i, 1).start()

    def stage_y2(i):
        for side in range(2):
            y1_copy(i, side).wait_recv()
            near = up if side == 0 else down
            for u in range(2):
                for half in range(2):
                    lanes = slice(half * HALF, (half + 1) * HALF)
                    value = s_sum[i, u, near, :, lanes]
                    if half == side:
                        value = value + y1_in[i, side, u]
                    y2_out[i, side, u, :, lanes] = value
            y2_copy(i, side).start()

    def stage_z(i):
        y2_copy(i, 0).wait_recv()
        y2_copy(i, 1).wait_recv()
        for u in range(2):
            value = s_sum[i, u, y] + y2_in[i, 0, u] + y2_in[i, 1, u]
            src, zz = piece(i, u)
            target = src * 2 + zz

            @pl.when(target != z)
            def _():
                r_out[i, u] = value
                z_copy(i, u, target).start()

            @pl.when(target == z)
            def _():
                r_own[i % NH] = value

    def compute(i):
        for side in range(2):
            src, zz = piece(i, side)
            for c in range(2):
                flag = a_flags[src * 4 + zz * 2 + c]
                kept = a_all[i, side, c].reshape(4 * SUB, CD) * flag
                hi = kept.astype(jnp.bfloat16)
                lo = (kept - hi.astype(jnp.float32)).astype(jnp.bfloat16)
                at = (side * 2 + c) * 4 * SUB
                a_hl[at : at + 4 * SUB, :] = hi
                a_hl[at + 16 * SUB : at + 20 * SUB, :] = lo

        @pl.loop(0, AB // 256)
        def _(n):
            lanes = pl.ds(pl.multiple_of(n * 256, 256), 256)
            both = jnp.dot(a_hl[...], v_hi[:, lanes], preferred_element_type=jnp.float32)
            low = jnp.dot(
                a_hl[0 : 16 * SUB, :], v_lo[:, lanes], preferred_element_type=jnp.float32
            )
            total = both[0 : 16 * SUB, :] + (both[16 * SUB :, :] + low)
            part[i, :, :, :, :, lanes] = total.reshape(2, 2, 4, SUB, 256)

        c_copy(i).start()

    @pl.loop(0, STEPS + 3)
    def _(i):
        @pl.when((i >= 1) & (i < STEPS + 1))
        def _():
            stage_y1(i - 1)

        @pl.when((i >= 2) & (i < STEPS + 2))
        def _():
            stage_y2(i - 2)

        @pl.when(i >= 3)
        def _():
            stage_z(i - 3)

        @pl.when(i < NH)
        def _():
            own_copy(i, 0).wait()
            own_copy(i, 1).wait()

        @pl.when((i >= NH) & (i < STEPS))
        def _():
            for side in range(2):
                pltpu.make_async_copy(
                    a_all.at[i, side], a_all.at[i, side], a_recv.at[side, i - NH]
                ).wait()

        @pl.when((i >= NH) & (i < 2 * NH))
        def _():
            a_forward(i - NH, 0).start()
            a_forward(i - NH, 1).start()

        @pl.when(i < STEPS)
        def _():
            compute(i)

    for h in range(NH):
        pltpu.make_async_copy(
            z_in.at[h, pl.ds(0, NZ - 1)], z_in.at[h, pl.ds(0, NZ - 1)], z_recv.at[h]
        ).wait()
        total = r_own[h]
        for k in range(NZ - 1):
            total = total + z_in[h, k]
        out[h * SUB : (h + 1) * SUB, :] = total

    for side in range(2):
        @pl.loop(0, 2 * NH)
        def _(j):
            pltpu.make_async_copy(
                a_all.at[NH + j, side], a_all.at[NH + j, side], a_send.at[side, j]
            ).wait()

        @pl.loop(0, NH)
        def _(j):
            a_forward(j, side).wait_send()

    @pl.loop(0, STEPS)
    def _(i):
        c_copy(i).wait_send()
        for side in range(2):
            y1_copy(i, side).wait_send()
            y2_copy(i, side).wait_send()
            src, zz = piece(i, side)
            target = src * 2 + zz

            @pl.when(target != z)
            def _():
                z_copy(i, side, target).wait_send()


def per_device(residual, amplitudes, integrals, t2_mask, v_mask):
    f32, bf16, dma = jnp.float32, jnp.bfloat16, pltpu.SemaphoreType.DMA
    summed = pl.pallas_call(
        kernel,
        out_shape=jax.ShapeDtypeStruct((32, AB), f32),
        in_specs=[pl.BlockSpec(memory_space=pl.ANY)] * 4,
        out_specs=pl.BlockSpec(memory_space=pltpu.VMEM),
        scratch_shapes=[
            pltpu.VMEM((STEPS, 2, 2, 4, SUB, CD), f32),
            pltpu.VMEM((CD, AB), f32),
            pltpu.VMEM((CD, AB), bf16),
            pltpu.VMEM((CD, AB), bf16),
            pltpu.VMEM((32 * SUB, CD), bf16),
            pltpu.VMEM((STEPS, 2, 2, 4, SUB, AB), f32),
            pltpu.VMEM((STEPS, 2, 4, SUB, AB), f32),
            pltpu.VMEM((STEPS, 2, 4, SUB, AB), f32),
            pltpu.VMEM((STEPS, 2, 2, SUB, HALF), f32),
            pltpu.VMEM((STEPS, 2, 2, SUB, AB), f32),
            pltpu.VMEM((STEPS, 2, 2, SUB, AB), f32),
            pltpu.VMEM((STEPS, 2, SUB, AB), f32),
            pltpu.VMEM((NH, SUB, AB), f32),
            pltpu.VMEM((NH, NZ - 1, SUB, AB), f32),
            pltpu.VMEM((NX, 4, 8), jnp.int32),
            pltpu.VMEM((8, 8), jnp.int32),
            pltpu.VMEM((16, 1, CD), f32),
            dma((2, 3 * NH)),
            dma((2, 3 * NH)),
            dma((NH, 2)),
            dma((8,)),
            dma((NX - 1,)),
            dma((NX - 1,)),
            dma((2,)),
            dma((STEPS,)),
            dma((STEPS,)),
            dma((2, STEPS)),
            dma((2, STEPS)),
            dma((2, STEPS)),
            dma((2, STEPS)),
            dma((2, STEPS)),
            dma((NH,)),
        ],
        compiler_params=pltpu.CompilerParams(
            collective_id=0, has_side_effects=True, vmem_limit_bytes=56 * 1024 * 1024
        ),
        name="ladder",
    )(amplitudes.reshape(2, 2, 4, 32, CD), integrals, t2_mask, v_mask)
    return residual + summed


def solution(mesh):
    in_specs = (
        P(("row", "depth"), "col"),
        P("col", ("row", "depth")),
        P(("row", "depth"), "col"),
        P("col", ("row", "depth")),
        P(("row", "depth"), "col"),
    )
    out_specs = P(("row", "depth"), "col")
    return jax.shard_map(
        per_device, mesh=mesh, in_specs=in_specs, out_specs=out_specs, check_vma=False
    )
```

```python
import jax
import jax.numpy as jnp
from jax import lax
from jax.experimental import pallas as pl
from jax.experimental.pallas import tpu as pltpu
from jax.sharding import PartitionSpec as P

TILE = 128
NX, NY, NZ = 4, 4, 8
SUB = 8
NH = 32 // SUB
NJ = 3 * NH
STEPS = NH + NJ
CD = 1024
AB = 1024
HALF = AB // 2
ROWS = 16 * SUB
MESH = pl.DeviceIdType.MESH

EARLY = 2
FWD = NH + EARLY


def expand_lanes(flags):
    values = flags.astype(jnp.float32)
    return jnp.concatenate(
        [jnp.broadcast_to(values[:, q : q + 1], (values.shape[0], TILE)) for q in range(8)],
        axis=1,
    )


def kernel(
    amp, integ, t2_mask, v_mask, out,
    a_all, v_f32, v_hi, v_lo, a_hl, part, c_in, s_sum, far_in, side_in, main_out, main_in,
    r_out, r_own, z_in, t2_all, v_flags, a_flags,
    a_send, a_recv, own_sem, v_sem, m_send, m_recv, m_sem, c_send, c_recv,
    far_send, far_recv, side_send, side_recv, main_send, main_recv, z_send, z_recv, z_known,
):
    row = lax.axis_index("row")
    x = lax.axis_index("col")
    y = lax.axis_index("depth")
    z = row // 2
    core = row % 2
    right, left = (x + 1) % NX, (x + 3) % NX
    up, down, far = (y + 1) % NY, (y + 3) % NY, (y + 2) % NY
    sibling = z * 2 + 1 - core
    z_next = ((z + 1) % NZ) * 2 + core
    z_prev = ((z + NZ - 1) % NZ) * 2 + core

    barrier = pltpu.get_barrier_semaphore()

    def greet(r, c, d):
        pl.semaphore_signal(barrier, inc=1, device_id=(r, c, d), device_id_type=MESH)

    greet(row, left, y)
    greet(row, right, y)
    greet(sibling, x, y)
    greet(row, x, up)
    greet(row, x, down)
    greet(z_next, x, y)
    greet(z_prev, x, y)

    def own_copy(h, zz):
        return pltpu.make_async_copy(
            amp.at[zz, :, :, pl.ds(h * SUB, SUB), :], a_all.at[h, zz], own_sem.at[h, zz]
        )

    def v_copy(q):
        block = pl.ds(q * TILE, TILE)
        return pltpu.make_async_copy(integ.at[block, :], v_f32.at[block, :], v_sem.at[q])

    m_copy = pltpu.make_async_copy(t2_mask, t2_all.at[x], m_sem.at[0])
    vm_copy = pltpu.make_async_copy(v_mask, v_flags, m_sem.at[1])
    vm_copy.start()
    for q in range(8):
        v_copy(q).start()
    m_copy.start()
    pl.semaphore_wait(barrier, 7)

    def a_own_send(j, zz, h, side):
        return pltpu.make_async_remote_copy(
            src_ref=amp.at[zz, :, :, pl.ds(h * SUB, SUB), :],
            dst_ref=a_all.at[NH + j, side],
            send_sem=a_send,
            recv_sem=a_recv.at[side, j],
            device_id=(row, right if side == 0 else left, y),
            device_id_type=MESH,
        )

    def a_forward(j, side):
        return pltpu.make_async_remote_copy(
            src_ref=a_all.at[NH + j, side],
            dst_ref=a_all.at[NH + FWD + j, side],
            send_sem=a_send,
            recv_sem=a_recv.at[side, FWD + j],
            device_id=(row, right if side == 0 else left, y),
            device_id_type=MESH,
        )

    def flag_send(src, who, k):
        return pltpu.make_async_remote_copy(
            src_ref=src,
            dst_ref=t2_all.at[who],
            send_sem=m_send.at[k],
            recv_sem=m_recv.at[k],
            device_id=(row, left if k == 1 else right, y),
            device_id_type=MESH,
        )

    for j in range(NH):
        for side in range(2):
            a_own_send(j, side, j, side).start()
    flag_send(t2_mask, x, 0).start()
    flag_send(t2_mask, x, 1).start()
    for j in range(EARLY):
        for side in range(2):
            a_own_send(NH + j, 1 - side, j, side).start()
    for h in range(NH):
        own_copy(h, 0).start()
        own_copy(h, 1).start()

    vm_copy.wait()
    flags_v = expand_lanes(v_flags[...])
    for q in range(8):
        v_copy(q).wait()
        rows = slice(q * TILE, (q + 1) * TILE)
        kept = v_f32[rows, :] * flags_v[q : q + 1, :]
        hi = kept.astype(jnp.bfloat16)
        v_hi[rows, :] = hi
        v_lo[rows, :] = (kept - hi.astype(jnp.float32)).astype(jnp.bfloat16)

    def widen(s):
        wide = expand_lanes(t2_all[s])
        for p in range(4):
            a_flags[s * 4 + p] = wide[p : p + 1, :]

    m_copy.wait()
    widen(x)

    def piece(i, side):
        second = ((i >= 2 * NH) & (i < 2 * NH + EARLY)) | (i >= 3 * NH + EARLY)
        forwarded = (i >= NH + FWD) & (i < 2 * NH + FWD)
        away = jnp.where(i < NH, 0, jnp.where(forwarded, 2, 1))
        zz = jnp.where(second, 1 - side, side)
        h = jnp.where(forwarded, i - NH - FWD, jnp.where(i >= 3 * NH + EARLY, i - 3 * NH, i % NH))
        src = (x + NX - away) % NX if side == 0 else (x + away) % NX
        return src, zz, h

    def c_copy(i, n):
        return pltpu.make_async_remote_copy(
            src_ref=part.at[i, n, :, 1 - core],
            dst_ref=c_in.at[i, n],
            send_sem=c_send,
            recv_sem=c_recv.at[n, i],
            device_id=(sibling, x, y),
            device_id_type=MESH,
        )

    def main_y(n):
        return up if n == 0 else down

    def side_y(n):
        return down if n == 0 else up

    def far_copy(i, n):
        return pltpu.make_async_remote_copy(
            src_ref=s_sum.at[i, n, far],
            dst_ref=far_in.at[i, n],
            send_sem=far_send,
            recv_sem=far_recv.at[n, i],
            device_id=(row, x, main_y(n)),
            device_id_type=MESH,
        )

    def side_copy(i, n):
        return pltpu.make_async_remote_copy(
            src_ref=s_sum.at[i, n, side_y(n)],
            dst_ref=side_in.at[i, n],
            send_sem=side_send,
            recv_sem=side_recv.at[n, i],
            device_id=(row, x, side_y(n)),
            device_id_type=MESH,
        )

    def main_copy(i, n):
        return pltpu.make_async_remote_copy(
            src_ref=main_out.at[i, n],
            dst_ref=main_in.at[i, n],
            send_sem=main_send,
            recv_sem=main_recv.at[n, i],
            device_id=(row, x, main_y(n)),
            device_id_type=MESH,
        )

    def z_copy(i, n, u, h, target):
        return pltpu.make_async_remote_copy(
            src_ref=r_out.at[i, n, u],
            dst_ref=z_in.at[h, n, (z + NZ - target + NZ - 1) % NZ],
            send_sem=z_send,
            recv_sem=z_recv.at[n, h],
            device_id=(target * 2 + core, x, y),
            device_id_type=MESH,
        )

    def stage_far(i, n):
        c_copy(i, n).wait_recv()
        for u in range(2):
            s_sum[i, n, :, u] = part[i, n, u, core] + c_in[i, n, u]
        far_copy(i, n).start()
        side_copy(i, n).start()

    def stage_main(i, n):
        far_copy(i, n).wait_recv()
        main_out[i, n] = s_sum[i, n, main_y(n)] + far_in[i, n]
        main_copy(i, n).start()

    def stage_z(i, n):
        side_copy(i, n).wait_recv()
        main_copy(i, n).wait_recv()
        value = s_sum[i, n, y] + side_in[i, n] + main_in[i, n]
        for u in range(2):
            src, zz, h = piece(i, u)
            target = src * 2 + zz

            @pl.when(target != z)
            def _():
                r_out[i, n, u] = value[u]
                z_copy(i, n, u, h, target).start()

            @pl.when(target == z)
            def _():
                r_own[h, n] = value[u]

    def compute(i):
        for side in range(2):
            src, zz, _ = piece(i, side)
            for c in range(2):
                flag = a_flags[src * 4 + zz * 2 + c]
                kept = a_all[i, side, c].reshape(4 * SUB, CD) * flag
                hi = kept.astype(jnp.bfloat16)
                lo = (kept - hi.astype(jnp.float32)).astype(jnp.bfloat16)
                at = (side * 2 + c) * 4 * SUB
                a_hl[at : at + 4 * SUB, :] = hi
                a_hl[at + ROWS : at + ROWS + 4 * SUB, :] = lo
        for n in range(2):
            for m in range(2):
                at = n * HALF + m * 256
                lanes = slice(at, at + 256)
                both = jnp.dot(a_hl[...], v_hi[:, lanes], preferred_element_type=jnp.float32)
                low = jnp.dot(
                    a_hl[0:ROWS, :], v_lo[:, lanes], preferred_element_type=jnp.float32
                )
                total = both[0:ROWS, :] + (both[ROWS:, :] + low)
                part[i, n, :, :, :, :, m * 256 : m * 256 + 256] = total.reshape(2, 2, 4, SUB, 256)
            c_copy(i, n).start()

    def know(r):
        pl.semaphore_signal(
            z_known.at[r, 0], inc=1, device_id=(z_next, x, y), device_id_type=MESH
        )
        pl.semaphore_signal(
            z_known.at[r, 1], inc=1, device_id=(z_prev, x, y), device_id_type=MESH
        )

    def known(r):
        pl.semaphore_wait(z_known.at[r, 0], 1)
        pl.semaphore_wait(z_known.at[r, 1], 1)

    @pl.loop(0, STEPS)
    def _(i):
        @pl.when(i < 3)
        def _():
            know(i)

        @pl.when(i >= 1)
        def _():
            stage_far(i - 1, 1)

        @pl.when(i >= 2)
        def _():
            stage_main(i - 2, 1)

        @pl.when(i >= 3)
        def _():
            stage_z(i - 3, 1)

        @pl.when(i < NH)
        def _():
            own_copy(i, 0).wait()
            own_copy(i, 1).wait()

        @pl.when(i == NH)
        def _():
            flag_send(t2_mask, x, 0).wait_recv()
            flag_send(t2_mask, x, 1).wait_recv()
            flag_send(t2_all.at[left], left, 2).start()
            widen(left)
            widen(right)

        @pl.when(i == NH + FWD)
        def _():
            flag_send(t2_all.at[left], left, 2).wait_recv()
            widen((x + 2) % NX)

        @pl.when(i >= NH)
        def _():
            for side in range(2):
                pltpu.make_async_copy(
                    a_all.at[i, side], a_all.at[i, side], a_recv.at[side, i - NH]
                ).wait()

        @pl.when((i >= NH) & (i < 2 * NH))
        def _():
            a_forward(i - NH, 0).start()
            a_forward(i - NH, 1).start()

        @pl.when(i == 2 * NH - 1)
        def _():
            for h in range(EARLY, NH):
                for side in range(2):
                    a_own_send(2 * NH + h, 1 - side, h, side).start()

        compute(i)

        @pl.when(i < 3)
        def _():
            known(i)

        stage_far(i, 0)

        @pl.when(i >= 1)
        def _():
            stage_main(i - 1, 0)

        @pl.when(i >= 2)
        def _():
            stage_z(i - 2, 0)

    last = STEPS - 1
    stage_main(last - 1, 1)
    stage_z(last - 2, 1)
    stage_far(last, 1)
    stage_z(last - 1, 0)
    stage_main(last, 0)
    stage_z(last - 1, 1)
    stage_main(last, 1)
    stage_z(last, 0)
    stage_z(last, 1)

    def all_of(ref, sem):
        pltpu.make_async_copy(ref, ref, sem).wait()

    all_of(a_all.at[pl.ds(NH, NJ)], a_send)
    all_of(c_in, c_send)
    all_of(far_in, far_send)
    all_of(side_in, side_send)
    all_of(main_in, main_send)
    all_of(z_in, z_send)
    for k in range(3):
        flag_send(t2_mask, x, k).wait_send()

    for h in range(NH):
        for n in range(2):
            all_of(z_in.at[h, n], z_recv.at[n, h])
            total = r_own[h, n]
            for k in range(NZ - 1):
                total = total + z_in[h, n, k]
            out[h * SUB : (h + 1) * SUB, n * HALF : (n + 1) * HALF] = total


def per_device(residual, amplitudes, integrals, t2_mask, v_mask):
    f32, bf16, dma = jnp.float32, jnp.bfloat16, pltpu.SemaphoreType.DMA
    summed = pl.pallas_call(
        kernel,
        out_shape=jax.ShapeDtypeStruct((32, AB), f32),
        in_specs=[pl.BlockSpec(memory_space=pl.ANY)] * 4,
        out_specs=pl.BlockSpec(memory_space=pltpu.VMEM),
        scratch_shapes=[
            pltpu.VMEM((STEPS, 2, 2, 4, SUB, CD), f32),
            pltpu.VMEM((CD, AB), f32),
            pltpu.VMEM((CD, AB), bf16),
            pltpu.VMEM((CD, AB), bf16),
            pltpu.VMEM((2 * ROWS, CD), bf16),
            pltpu.VMEM((STEPS, 2, 2, 2, 4, SUB, HALF), f32),
            pltpu.VMEM((STEPS, 2, 2, 4, SUB, HALF), f32),
            pltpu.VMEM((STEPS, 2, 4, 2, SUB, HALF), f32),
            pltpu.VMEM((STEPS, 2, 2, SUB, HALF), f32),
            pltpu.VMEM((STEPS, 2, 2, SUB, HALF), f32),
            pltpu.VMEM((STEPS, 2, 2, SUB, HALF), f32),
            pltpu.VMEM((STEPS, 2, 2, SUB, HALF), f32),
            pltpu.VMEM((STEPS, 2, 2, SUB, HALF), f32),
            pltpu.VMEM((NH, 2, SUB, HALF), f32),
            pltpu.VMEM((NH, 2, NZ - 1, SUB, HALF), f32),
            pltpu.VMEM((NX, 4, 8), jnp.int32),
            pltpu.VMEM((8, 8), jnp.int32),
            pltpu.VMEM((16, 1, CD), f32),
            dma(()),
            dma((2, NJ)),
            dma((NH, 2)),
            dma((8,)),
            dma((3,)),
            dma((3,)),
            dma((2,)),
            dma(()),
            dma((2, STEPS)),
            dma(()),
            dma((2, STEPS)),
            dma(()),
            dma((2, STEPS)),
            dma(()),
            dma((2, STEPS)),
            dma(()),
            dma((2, NH)),
            pltpu.SemaphoreType.REGULAR((3, 2)),
        ],
        compiler_params=pltpu.CompilerParams(
            collective_id=0, has_side_effects=True, vmem_limit_bytes=56 * 1024 * 1024
        ),
        name="ladder",
    )(amplitudes.reshape(2, 2, 4, 32, CD), integrals, t2_mask, v_mask)
    return residual + summed


def solution(mesh):
    in_specs = (
        P(("row", "depth"), "col"),
        P("col", ("row", "depth")),
        P(("row", "depth"), "col"),
        P("col", ("row", "depth")),
        P(("row", "depth"), "col"),
    )
    out_specs = P(("row", "depth"), "col")
    return jax.shard_map(
        per_device, mesh=mesh, in_specs=in_specs, out_specs=out_specs, check_vma=False
    )
```

```python
import jax
import jax.numpy as jnp
from jax import lax
from jax.experimental import pallas as pl
from jax.experimental.pallas import tpu as pltpu
from jax.sharding import PartitionSpec as P

TILE = 128
NX, NY, NZ = 4, 4, 8
SUB = 16
NQ = 32 // SUB
NK = NY * NQ
NJ = 3 * NK
STEPS = NK + NJ
CD = 1024
AB = 1024
HALF = AB // 2
ROWS = 4 * SUB
MESH = pl.DeviceIdType.MESH
LAG = 1
LATE = 28


def expand_lanes(flags):
    values = flags.astype(jnp.float32)
    return jnp.concatenate(
        [jnp.broadcast_to(values[:, q : q + 1], (values.shape[0], TILE)) for q in range(8)],
        axis=1,
    )


def kernel(
    amp, integ, t2_mask, v_mask, out,
    a_all, v_f32, v_hi, v_lo, a_hl, part, c_in, s_out, far_in, near_in,
    r_own, z_in, t2_all, v_flags, a_flags,
    a_send, a_recv, own_sem, v_sem, m_send, m_recv, m_sem, c_send, c_recv,
    far_send, far_recv, near_send, near_recv, z_send, z_recv, z_known,
):
    row = lax.axis_index("row")
    x = lax.axis_index("col")
    y = lax.axis_index("depth")
    z = row // 2
    core = row % 2
    right, left = (x + 1) % NX, (x + 3) % NX
    up, down = (y + 1) % NY, (y + 3) % NY
    sibling = z * 2 + 1 - core
    z_next = ((z + 1) % NZ) * 2 + core
    z_prev = ((z + NZ - 1) % NZ) * 2 + core

    barrier = pltpu.get_barrier_semaphore()

    def greet(r, c, d):
        pl.semaphore_signal(barrier, inc=1, device_id=(r, c, d), device_id_type=MESH)

    greet(row, left, y)
    greet(row, right, y)
    greet(sibling, x, y)
    greet(row, x, up)
    greet(row, x, down)
    greet(z_next, x, y)
    greet(z_prev, x, y)

    def rows_of(k, side):
        middle = (k >= NQ) & (k < 3 * NQ)
        turn = (k + NQ + side) % 2
        kind = jnp.where(k < NQ, 0, jnp.where(middle, 1 + turn, 3))
        owner = (y + jnp.where(k < NQ, 2, jnp.where(middle, 1 + 2 * turn, 0))) % NY
        part_of = jnp.where(middle, (k + NQ) // 2 % NQ, k % NQ)
        return kind, owner, part_of

    block = z // 2
    turn_in = (x + NX - 1 - block) % NX, (x + 1 + NX - block) % NX
    turn_out = (x + NX - block) % NX
    f_last = (
        (turn_in[0] == 1) | (turn_in[0] == 2),
        (turn_in[1] == 3) | (turn_in[1] == 2),
    )
    f_last_out = (turn_out == 1) | (turn_out == 2), (turn_out == 3) | (turn_out == 2)

    def b_slot(k, side):
        late = 0 if k < NK // 2 else jnp.where(f_last_out[side], 0, NK)
        return NK + k + late

    def f_slot(k, side):
        return k + jnp.where(f_last_out[side], 2 * NK, NK + NK // 2)

    def piece(t, side):
        j = t - NK
        split_b = jnp.where(j < NK + NK // 2, 2, jnp.where(j < 2 * NK + NK // 2, 3, 2))
        split_k = jnp.where(
            j < NK + NK // 2, j - NK, jnp.where(j < 2 * NK + NK // 2, j - NK - NK // 2, j - 2 * NK)
        )
        whole_b = jnp.where(j < 2 * NK, 2, 3)
        whole_k = jnp.where(j < 2 * NK, j - NK, j - 2 * NK)
        later_g = jnp.where(f_last[side], whole_b, split_b)
        later_k = jnp.where(f_last[side], whole_k, split_k)
        g = jnp.where(t < NK, 0, jnp.where(j < NK, 1, later_g))
        k = jnp.where(t < NK, t, jnp.where(j < NK, j, later_k))
        away = jnp.where(g == 0, 0, jnp.where(g == 3, 2, 1))
        zz = jnp.where(g == 2, 1 - side, side)
        src = (x + NX - away) % NX if side == 0 else (x + away) % NX
        return src, zz, g, k

    def own_copy(k, zz):
        _, owner, half = rows_of(k, zz)
        return pltpu.make_async_copy(
            amp.at[zz, :, owner, half], a_all.at[k, zz], own_sem.at[zz, k]
        )

    def v_copy(q):
        at = pl.ds(q * TILE, TILE)
        return pltpu.make_async_copy(integ.at[at, :], v_f32.at[at, :], v_sem.at[q])

    m_copy = pltpu.make_async_copy(t2_mask, t2_all.at[x], m_sem.at[0])
    vm_copy = pltpu.make_async_copy(v_mask, v_flags, m_sem.at[1])
    vm_copy.start()
    for q in range(8):
        v_copy(q).start()
    m_copy.start()
    pl.semaphore_wait(barrier, 7)

    def a_own_send(slot, zz, k, side):
        _, owner, half = rows_of(k, side)
        return pltpu.make_async_remote_copy(
            src_ref=amp.at[zz, :, owner, half],
            dst_ref=a_all.at[NK + slot, side],
            send_sem=a_send,
            recv_sem=a_recv.at[side, slot],
            device_id=(row, right if side == 0 else left, y),
            device_id_type=MESH,
        )

    def a_forward(k, side):
        slot = f_slot(k, side)
        return pltpu.make_async_remote_copy(
            src_ref=a_all.at[NK + k, side],
            dst_ref=a_all.at[NK + slot, side],
            send_sem=a_send,
            recv_sem=a_recv.at[side, slot],
            device_id=(row, right if side == 0 else left, y),
            device_id_type=MESH,
        )

    def flag_send(src, who, k):
        return pltpu.make_async_remote_copy(
            src_ref=src,
            dst_ref=t2_all.at[who],
            send_sem=m_send.at[k],
            recv_sem=m_recv.at[k],
            device_id=(row, left if k == 1 else right, y),
            device_id_type=MESH,
        )

    for k in range(NK):
        for side in range(2):
            a_own_send(k, side, k, side).start()
    flag_send(t2_mask, x, 0).start()
    flag_send(t2_mask, x, 1).start()
    for k in range(NK):
        own_copy(k, 0).start()
        own_copy(k, 1).start()
    for k in range(NK // 2):
        for side in range(2):
            a_own_send(b_slot(k, side), 1 - side, k, side).start()
    for side in range(2):
        @pl.when(f_last_out[side])
        def _():
            for k in range(NK // 2, NK):
                a_own_send(b_slot(k, side), 1 - side, k, side).start()

    vm_copy.wait()
    flags_v = expand_lanes(v_flags[...])
    for q in range(8):
        v_copy(q).wait()
        rows = slice(q * TILE, (q + 1) * TILE)
        kept = v_f32[rows, :] * flags_v[q : q + 1, :]
        hi = kept.astype(jnp.bfloat16)
        v_hi[rows, :] = hi
        v_lo[rows, :] = (kept - hi.astype(jnp.float32)).astype(jnp.bfloat16)

    def widen(s):
        wide = expand_lanes(t2_all[s])
        for p in range(4):
            a_flags[s * 4 + p] = wide[p : p + 1, :]

    m_copy.wait()
    widen(x)

    def c_copy(t):
        return pltpu.make_async_remote_copy(
            src_ref=part.at[t, :, 1 - core],
            dst_ref=c_in.at[t],
            send_sem=c_send,
            recv_sem=c_recv.at[t],
            device_id=(sibling, x, y),
            device_id_type=MESH,
        )

    def far_copy(t, u, g, half, way):
        return pltpu.make_async_remote_copy(
            src_ref=s_out.at[t, u, :, pl.ds(way * HALF, HALF)],
            dst_ref=far_in.at[g, u, half, way],
            send_sem=far_send,
            recv_sem=far_recv.at[g, u * 2 * NQ + half * 2 + way],
            device_id=(row, x, up if way == 0 else down),
            device_id_type=MESH,
        )

    def near_copy(t, u, g, half, way):
        return pltpu.make_async_remote_copy(
            src_ref=s_out.at[t, u],
            dst_ref=near_in.at[g, u, half, way],
            send_sem=near_send,
            recv_sem=near_recv.at[g, u * 2 * NQ + half * 2 + way],
            device_id=(row, x, up if way == 0 else down),
            device_id_type=MESH,
        )

    def z_copy(t, u, half, target):
        return pltpu.make_async_remote_copy(
            src_ref=s_out.at[t, u],
            dst_ref=z_in.at[half, (z + NZ - target + NZ - 1) % NZ],
            send_sem=z_send,
            recv_sem=z_recv.at[half],
            device_id=(target * 2 + core, x, y),
            device_id_type=MESH,
        )

    def settle(t):
        c_copy(t).wait_recv()
        for u in range(2):
            src, zz, g, k = piece(t, u)
            kind, _, half = rows_of(k, u)

            @pl.when(kind == 0)
            def _():
                s_out[t, u] = part[t, u, core] + c_in[t, u]
                far_copy(t, u, g, half, 0).start()
                far_copy(t, u, g, half, 1).start()

            for way in range(2):
                @pl.when(kind == 1 + way)
                def _():
                    far_copy(t, u, g, half, way).wait_recv()
                    for w in range(2):
                        lanes = slice(w * HALF, (w + 1) * HALF)
                        value = part[t, u, core, :, lanes] + c_in[t, u, :, lanes]
                        if w == way:
                            value = value + far_in[g, u, half, way]
                        s_out[t, u, :, lanes] = value
                    near_copy(t, u, g, half, way).start()

            @pl.when(kind == 3)
            def _():
                near_copy(t, u, g, half, 0).wait_recv()
                near_copy(t, u, g, half, 1).wait_recv()
                value = part[t, u, core] + c_in[t, u]
                value = value + (near_in[g, u, half, 0] + near_in[g, u, half, 1])
                target = src * 2 + zz

                @pl.when(target != z)
                def _():
                    s_out[t, u] = value
                    z_copy(t, u, half, target).start()

                @pl.when(target == z)
                def _():
                    r_own[half] = value

    def compute(t):
        for side in range(2):
            src, zz, _, _ = piece(t, side)
            for c in range(2):
                kept = a_all[t, side, c] * a_flags[src * 4 + zz * 2 + c]
                hi = kept.astype(jnp.bfloat16)
                lo = (kept - hi.astype(jnp.float32)).astype(jnp.bfloat16)
                at = (side * 2 + c) * SUB
                a_hl[at : at + SUB, :] = hi
                a_hl[at + ROWS : at + ROWS + SUB, :] = lo
        for m in range(AB // 256):
            lanes = slice(m * 256, m * 256 + 256)
            both = jnp.dot(a_hl[...], v_hi[:, lanes], preferred_element_type=jnp.float32)
            low = jnp.dot(a_hl[0:ROWS, :], v_lo[:, lanes], preferred_element_type=jnp.float32)
            total = both[0:ROWS, :] + (both[ROWS:, :] + low)
            part[t, :, :, :, lanes] = total.reshape(2, 2, SUB, 256)
        c_copy(t).start()

    def know(r):
        for way, who in ((0, z_next), (1, z_prev)):
            pl.semaphore_signal(
                z_known.at[r, way], inc=1, device_id=(who, x, y), device_id_type=MESH
            )

    def known(r):
        pl.semaphore_wait(z_known.at[r, 0], 1)
        pl.semaphore_wait(z_known.at[r, 1], 1)

    @pl.loop(0, STEPS)
    def _(t):
        for r in range(3):
            @pl.when(t == 2 * r)
            def _():
                if r > 0:
                    known(r - 1)
                know(r)

        @pl.when(t == NK - 2)
        def _():
            known(2)

        @pl.when(t >= LATE)
        def _():
            settle(t - LAG)

        @pl.when(t < NK)
        def _():
            own_copy(t, 0).wait()
            own_copy(t, 1).wait()

        @pl.when(t == NK)
        def _():
            flag_send(t2_mask, x, 0).wait_recv()
            flag_send(t2_mask, x, 1).wait_recv()
            flag_send(t2_all.at[left], left, 2).start()
            widen(left)
            widen(right)

        @pl.when(t == 2 * NK + NK // 2)
        def _():
            flag_send(t2_all.at[left], left, 2).wait_recv()
            widen((x + 2) % NX)

        @pl.when(t >= NK)
        def _():
            for side in range(2):
                pltpu.make_async_copy(
                    a_all.at[t, side], a_all.at[t, side], a_recv.at[side, t - NK]
                ).wait()

        @pl.when((t >= NK) & (t < 2 * NK))
        def _():
            a_forward(t - NK, 0).start()
            a_forward(t - NK, 1).start()

        for side in range(2):
            @pl.when((t == 2 * NK - 1) & jnp.logical_not(f_last_out[side]))
            def _():
                for k in range(NK // 2, NK):
                    a_own_send(b_slot(k, side), 1 - side, k, side).start()

        compute(t)

        @pl.when((t >= LAG) & (t < LATE))
        def _():
            settle(t - LAG)

    for t in range(STEPS - LAG, STEPS):
        settle(t)

    def all_of(ref, sem):
        pltpu.make_async_copy(ref, ref, sem).wait()

    all_of(a_all.at[pl.ds(NK, NJ)], a_send)
    all_of(c_in, c_send)
    all_of(far_in, far_send)
    all_of(near_in, near_send)
    all_of(z_in, z_send)
    for k in range(3):
        flag_send(t2_mask, x, k).wait_send()

    for half in range(NQ):
        all_of(z_in.at[half], z_recv.at[half])
        total = r_own[half]
        for k in range(NZ - 1):
            total = total + z_in[half, k]
        out[half * SUB : (half + 1) * SUB, :] = total


def per_device(residual, amplitudes, integrals, t2_mask, v_mask):
    f32, bf16, dma = jnp.float32, jnp.bfloat16, pltpu.SemaphoreType.DMA
    summed = pl.pallas_call(
        kernel,
        out_shape=jax.ShapeDtypeStruct((32, AB), f32),
        in_specs=[pl.BlockSpec(memory_space=pl.ANY)] * 4,
        out_specs=pl.BlockSpec(memory_space=pltpu.VMEM),
        scratch_shapes=[
            pltpu.VMEM((STEPS, 2, 2, SUB, CD), f32),
            pltpu.VMEM((CD, AB), f32),
            pltpu.VMEM((CD, AB), bf16),
            pltpu.VMEM((CD, AB), bf16),
            pltpu.VMEM((2 * ROWS, CD), bf16),
            pltpu.VMEM((STEPS, 2, 2, SUB, AB), f32),
            pltpu.VMEM((STEPS, 2, SUB, AB), f32),
            pltpu.VMEM((STEPS, 2, SUB, AB), f32),
            pltpu.VMEM((4, 2, NQ, 2, SUB, HALF), f32),
            pltpu.VMEM((4, 2, NQ, 2, SUB, AB), f32),
            pltpu.VMEM((NQ, SUB, AB), f32),
            pltpu.VMEM((NQ, NZ - 1, SUB, AB), f32),
            pltpu.VMEM((NX, 4, 8), jnp.int32),
            pltpu.VMEM((8, 8), jnp.int32),
            pltpu.VMEM((16, 1, CD), f32),
            dma(()),
            dma((2, NJ)),
            dma((2, NK)),
            dma((8,)),
            dma((3,)),
            dma((3,)),
            dma((2,)),
            dma(()),
            dma((STEPS,)),
            dma(()),
            dma((4, 4 * NQ)),
            dma(()),
            dma((4, 4 * NQ)),
            dma(()),
            dma((NQ,)),
            pltpu.SemaphoreType.REGULAR((3, 2)),
        ],
        compiler_params=pltpu.CompilerParams(
            collective_id=0, has_side_effects=True, vmem_limit_bytes=56 * 1024 * 1024
        ),
        name="ladder",
    )(amplitudes.reshape(2, 2, NY, NQ, SUB, CD), integrals, t2_mask, v_mask)
    return residual + summed


def solution(mesh):
    in_specs = (
        P(("row", "depth"), "col"),
        P("col", ("row", "depth")),
        P(("row", "depth"), "col"),
        P("col", ("row", "depth")),
        P(("row", "depth"), "col"),
    )
    out_specs = P(("row", "depth"), "col")
    return jax.shard_map(
        per_device, mesh=mesh, in_specs=in_specs, out_specs=out_specs, check_vma=False
    )
```

```python
import jax
import jax.numpy as jnp
from jax import lax
from jax.experimental import pallas as pl
from jax.experimental.pallas import tpu as pltpu
from jax.sharding import PartitionSpec as P

TILE = 128
NX, NY, NZ = 4, 4, 8
SUB = 16
NQ = 32 // SUB
NK = NY * NQ
NJ = 3 * NK
STEPS = NK + NJ
CD = 1024
AB = 1024
HALF = AB // 2
ROWS = 4 * SUB
MESH = pl.DeviceIdType.MESH
LAG = 1
LATE = 28
BODY = STEPS - 2
FINE = SUB // 2


def expand_lanes(flags):
    values = flags.astype(jnp.float32)
    return jnp.concatenate(
        [jnp.broadcast_to(values[:, q : q + 1], (values.shape[0], TILE)) for q in range(8)],
        axis=1,
    )


def kernel(
    amp, integ, t2_mask, v_mask, out,
    a_all, v_f32, v_hi, v_lo, a_hl, part, c_in, s_out, far_in, near_in,
    r_own, z_in, t2_all, v_flags, a_flags,
    a_send, a_recv, own_sem, v_sem, m_send, m_recv, m_sem, c_send, c_recv,
    far_send, far_recv, near_send, near_recv, z_send, z_recv, z_known, fine_recv, c_fine_recv,
):
    row = lax.axis_index("row")
    x = lax.axis_index("col")
    y = lax.axis_index("depth")
    z = row // 2
    core = row % 2
    right, left = (x + 1) % NX, (x + 3) % NX
    up, down = (y + 1) % NY, (y + 3) % NY
    sibling = z * 2 + 1 - core
    z_next = ((z + 1) % NZ) * 2 + core
    z_prev = ((z + NZ - 1) % NZ) * 2 + core

    barrier = pltpu.get_barrier_semaphore()

    def greet(r, c, d):
        pl.semaphore_signal(barrier, inc=1, device_id=(r, c, d), device_id_type=MESH)

    greet(row, left, y)
    greet(row, right, y)
    greet(sibling, x, y)
    greet(row, x, up)
    greet(row, x, down)
    greet(z_next, x, y)
    greet(z_prev, x, y)

    def rows_of(k, side):
        middle = (k >= NQ) & (k < 3 * NQ)
        turn = (k + NQ + side) % 2
        kind = jnp.where(k < NQ, 0, jnp.where(middle, 1 + turn, 3))
        owner = (y + jnp.where(k < NQ, 2, jnp.where(middle, 1 + 2 * turn, 0))) % NY
        part_of = jnp.where(middle, (k + NQ) // 2 % NQ, k % NQ)
        return kind, owner, part_of

    block = z // 2
    turn_in = (x + NX - 1 - block) % NX, (x + 1 + NX - block) % NX
    turn_out = (x + NX - block) % NX
    f_last = (
        (turn_in[0] == 1) | (turn_in[0] == 2),
        (turn_in[1] == 3) | (turn_in[1] == 2),
    )
    f_last_out = (turn_out == 1) | (turn_out == 2), (turn_out == 3) | (turn_out == 2)

    def b_slot(k, side):
        late = 0 if k < NK // 2 else jnp.where(f_last_out[side], 0, NK)
        return NK + k + late

    def f_slot(k, side):
        return k + jnp.where(f_last_out[side], 2 * NK, NK + NK // 2)

    def piece(t, side):
        j = t - NK
        split_b = jnp.where(j < NK + NK // 2, 2, jnp.where(j < 2 * NK + NK // 2, 3, 2))
        split_k = jnp.where(
            j < NK + NK // 2, j - NK, jnp.where(j < 2 * NK + NK // 2, j - NK - NK // 2, j - 2 * NK)
        )
        whole_b = jnp.where(j < 2 * NK, 2, 3)
        whole_k = jnp.where(j < 2 * NK, j - NK, j - 2 * NK)
        later_g = jnp.where(f_last[side], whole_b, split_b)
        later_k = jnp.where(f_last[side], whole_k, split_k)
        g = jnp.where(t < NK, 0, jnp.where(j < NK, 1, later_g))
        k = jnp.where(t < NK, t, jnp.where(j < NK, j, later_k))
        away = jnp.where(g == 0, 0, jnp.where(g == 3, 2, 1))
        zz = jnp.where(g == 2, 1 - side, side)
        src = (x + NX - away) % NX if side == 0 else (x + away) % NX
        return src, zz, g, k

    def own_copy(k, zz):
        _, owner, half = rows_of(k, zz)
        return pltpu.make_async_copy(
            amp.at[zz, :, owner, half], a_all.at[k, zz], own_sem.at[zz, k]
        )

    def v_copy(q):
        at = pl.ds(q * TILE, TILE)
        return pltpu.make_async_copy(integ.at[at, :], v_f32.at[at, :], v_sem.at[q])

    m_copy = pltpu.make_async_copy(t2_mask, t2_all.at[x], m_sem.at[0])
    vm_copy = pltpu.make_async_copy(v_mask, v_flags, m_sem.at[1])
    vm_copy.start()
    for q in range(8):
        v_copy(q).start()
    m_copy.start()
    pl.semaphore_wait(barrier, 7)

    def a_own_send(slot, zz, k, side):
        _, owner, half = rows_of(k, side)
        return pltpu.make_async_remote_copy(
            src_ref=amp.at[zz, :, owner, half],
            dst_ref=a_all.at[NK + slot, side],
            send_sem=a_send,
            recv_sem=a_recv.at[side, slot],
            device_id=(row, right if side == 0 else left, y),
            device_id_type=MESH,
        )

    def a_own_fine(zz, k, side, e):
        _, owner, half = rows_of(k, side)
        rows = pl.ds(e * FINE, FINE)
        return pltpu.make_async_remote_copy(
            src_ref=amp.at[zz, :, owner, half, rows],
            dst_ref=a_all.at[STEPS - NK + k, side, :, rows],
            send_sem=a_send,
            recv_sem=fine_recv.at[side, (k - NK + 2) * 2 + e],
            device_id=(row, right if side == 0 else left, y),
            device_id_type=MESH,
        )

    def a_forward_fine(k, side, e):
        rows = pl.ds(e * FINE, FINE)
        return pltpu.make_async_remote_copy(
            src_ref=a_all.at[NK + k, side, :, rows],
            dst_ref=a_all.at[STEPS - NK + k, side, :, rows],
            send_sem=a_send,
            recv_sem=fine_recv.at[side, (k - NK + 2) * 2 + e],
            device_id=(row, right if side == 0 else left, y),
            device_id_type=MESH,
        )

    def a_forward(k, side):
        slot = f_slot(k, side)
        return pltpu.make_async_remote_copy(
            src_ref=a_all.at[NK + k, side],
            dst_ref=a_all.at[NK + slot, side],
            send_sem=a_send,
            recv_sem=a_recv.at[side, slot],
            device_id=(row, right if side == 0 else left, y),
            device_id_type=MESH,
        )

    def flag_send(src, who, k):
        return pltpu.make_async_remote_copy(
            src_ref=src,
            dst_ref=t2_all.at[who],
            send_sem=m_send.at[k],
            recv_sem=m_recv.at[k],
            device_id=(row, left if k == 1 else right, y),
            device_id_type=MESH,
        )

    for k in range(NK):
        for side in range(2):
            a_own_send(k, side, k, side).start()
    flag_send(t2_mask, x, 0).start()
    flag_send(t2_mask, x, 1).start()
    for k in range(NK):
        own_copy(k, 0).start()
        own_copy(k, 1).start()
    for k in range(NK // 2):
        for side in range(2):
            a_own_send(b_slot(k, side), 1 - side, k, side).start()
    for side in range(2):
        @pl.when(f_last_out[side])
        def _():
            for k in range(NK // 2, NK):
                a_own_send(b_slot(k, side), 1 - side, k, side).start()

    vm_copy.wait()
    flags_v = expand_lanes(v_flags[...])
    for q in range(8):
        v_copy(q).wait()
        rows = slice(q * TILE, (q + 1) * TILE)
        kept = v_f32[rows, :] * flags_v[q : q + 1, :]
        hi = kept.astype(jnp.bfloat16)
        v_hi[rows, :] = hi
        v_lo[rows, :] = (kept - hi.astype(jnp.float32)).astype(jnp.bfloat16)

    def widen(s):
        wide = expand_lanes(t2_all[s])
        for p in range(4):
            a_flags[s * 4 + p] = wide[p : p + 1, :]

    m_copy.wait()
    widen(x)

    def c_copy(t):
        return pltpu.make_async_remote_copy(
            src_ref=part.at[t, :, 1 - core],
            dst_ref=c_in.at[t],
            send_sem=c_send,
            recv_sem=c_recv.at[t],
            device_id=(sibling, x, y),
            device_id_type=MESH,
        )

    def far_copy(t, u, g, half, way):
        return pltpu.make_async_remote_copy(
            src_ref=s_out.at[t, u, :, pl.ds(way * HALF, HALF)],
            dst_ref=far_in.at[g, u, half, way],
            send_sem=far_send,
            recv_sem=far_recv.at[g, u * 2 * NQ + half * 2 + way],
            device_id=(row, x, up if way == 0 else down),
            device_id_type=MESH,
        )

    def near_copy(t, u, g, half, way):
        return pltpu.make_async_remote_copy(
            src_ref=s_out.at[t, u],
            dst_ref=near_in.at[g, u, half, way],
            send_sem=near_send,
            recv_sem=near_recv.at[g, u * 2 * NQ + half * 2 + way],
            device_id=(row, x, up if way == 0 else down),
            device_id_type=MESH,
        )

    def z_copy(t, u, half, target):
        return pltpu.make_async_remote_copy(
            src_ref=s_out.at[t, u],
            dst_ref=z_in.at[half, (z + NZ - target + NZ - 1) % NZ],
            send_sem=z_send,
            recv_sem=z_recv.at[half],
            device_id=(target * 2 + core, x, y),
            device_id_type=MESH,
        )

    def settle(t):
        c_copy(t).wait_recv()
        for u in range(2):
            src, zz, g, k = piece(t, u)
            kind, _, half = rows_of(k, u)

            @pl.when(kind == 0)
            def _():
                s_out[t, u] = part[t, u, core] + c_in[t, u]
                far_copy(t, u, g, half, 0).start()
                far_copy(t, u, g, half, 1).start()

            for way in range(2):
                @pl.when(kind == 1 + way)
                def _():
                    far_copy(t, u, g, half, way).wait_recv()
                    for w in range(2):
                        lanes = slice(w * HALF, (w + 1) * HALF)
                        value = part[t, u, core, :, lanes] + c_in[t, u, :, lanes]
                        if w == way:
                            value = value + far_in[g, u, half, way]
                        s_out[t, u, :, lanes] = value
                    near_copy(t, u, g, half, way).start()

            @pl.when(kind == 3)
            def _():
                near_copy(t, u, g, half, 0).wait_recv()
                near_copy(t, u, g, half, 1).wait_recv()
                value = part[t, u, core] + c_in[t, u]
                value = value + (near_in[g, u, half, 0] + near_in[g, u, half, 1])
                target = src * 2 + zz

                @pl.when(target != z)
                def _():
                    s_out[t, u] = value
                    z_copy(t, u, half, target).start()

                @pl.when(target == z)
                def _():
                    r_own[half] = value

    def compute(t):
        for side in range(2):
            src, zz, _, _ = piece(t, side)
            for c in range(2):
                kept = a_all[t, side, c] * a_flags[src * 4 + zz * 2 + c]
                hi = kept.astype(jnp.bfloat16)
                lo = (kept - hi.astype(jnp.float32)).astype(jnp.bfloat16)
                at = (side * 2 + c) * SUB
                a_hl[at : at + SUB, :] = hi
                a_hl[at + ROWS : at + ROWS + SUB, :] = lo
        for m in range(AB // 256):
            lanes = slice(m * 256, m * 256 + 256)
            both = jnp.dot(a_hl[...], v_hi[:, lanes], preferred_element_type=jnp.float32)
            low = jnp.dot(a_hl[0:ROWS, :], v_lo[:, lanes], preferred_element_type=jnp.float32)
            total = both[0:ROWS, :] + (both[ROWS:, :] + low)
            part[t, :, :, :, lanes] = total.reshape(2, 2, SUB, 256)
        c_copy(t).start()

    def know(r):
        for way, who in ((0, z_next), (1, z_prev)):
            pl.semaphore_signal(
                z_known.at[r, way], inc=1, device_id=(who, x, y), device_id_type=MESH
            )

    def known(r):
        pl.semaphore_wait(z_known.at[r, 0], 1)
        pl.semaphore_wait(z_known.at[r, 1], 1)

    @pl.loop(0, BODY)
    def _(t):
        for r in range(3):
            @pl.when(t == 2 * r)
            def _():
                if r > 0:
                    known(r - 1)
                know(r)

        @pl.when(t == NK - 2)
        def _():
            known(2)

        @pl.when(t >= LATE)
        def _():
            settle(t - LAG)

        @pl.when(t < NK)
        def _():
            own_copy(t, 0).wait()
            own_copy(t, 1).wait()

        @pl.when(t == NK)
        def _():
            flag_send(t2_mask, x, 0).wait_recv()
            flag_send(t2_mask, x, 1).wait_recv()
            flag_send(t2_all.at[left], left, 2).start()
            widen(left)
            widen(right)

        @pl.when(t == 2 * NK + NK // 2)
        def _():
            flag_send(t2_all.at[left], left, 2).wait_recv()
            widen((x + 2) % NX)

        @pl.when(t >= NK)
        def _():
            for side in range(2):
                pltpu.make_async_copy(
                    a_all.at[t, side], a_all.at[t, side], a_recv.at[side, t - NK]
                ).wait()

        @pl.when((t >= NK) & (t < 2 * NK))
        def _():
            for side in range(2):
                fine = f_last_out[side] & (t >= 2 * NK - 2)

                @pl.when(jnp.logical_not(fine))
                def _():
                    a_forward(t - NK, side).start()

                @pl.when(fine)
                def _():
                    for e in range(2):
                        a_forward_fine(t - NK, side, e).start()

        for side in range(2):
            @pl.when((t == 2 * NK - 1) & jnp.logical_not(f_last_out[side]))
            def _():
                for k in range(NK // 2, NK - 2):
                    a_own_send(b_slot(k, side), 1 - side, k, side).start()
                for k in range(NK - 2, NK):
                    for e in range(2):
                        a_own_fine(1 - side, k, side, e).start()

        compute(t)

        @pl.when((t >= LAG) & (t < LATE))
        def _():
            settle(t - LAG)

    settle(BODY - 1)

    def c_fine(q):
        rows = pl.ds(q % 2 * FINE, FINE)
        return pltpu.make_async_remote_copy(
            src_ref=part.at[BODY + q // 2, :, 1 - core, rows],
            dst_ref=c_in.at[BODY + q // 2, :, rows],
            send_sem=c_send,
            recv_sem=c_fine_recv.at[q],
            device_id=(sibling, x, y),
            device_id_type=MESH,
        )

    def compute_fine(q):
        t, rows = BODY + q // 2, slice(q % 2 * FINE, q % 2 * FINE + FINE)
        kept = []
        for side in range(2):
            src, zz, _, _ = piece(t, side)
            for c in range(2):
                kept.append(a_all[t, side, c, rows, :] * a_flags[src * 4 + zz * 2 + c])
        kept = jnp.concatenate(kept, axis=0)
        hi = kept.astype(jnp.bfloat16)
        lo = (kept - hi.astype(jnp.float32)).astype(jnp.bfloat16)
        n = 4 * FINE
        a_hl[0:n, :] = hi
        a_hl[n : 2 * n, :] = lo
        for m in range(AB // 256):
            lanes = slice(m * 256, m * 256 + 256)
            both = jnp.dot(a_hl[0 : 2 * n, :], v_hi[:, lanes], preferred_element_type=jnp.float32)
            low = jnp.dot(a_hl[0:n, :], v_lo[:, lanes], preferred_element_type=jnp.float32)
            total = both[0:n, :] + (both[n:, :] + low)
            part[t, :, :, rows, lanes] = total.reshape(2, 2, FINE, 256)
        c_fine(q).start()

    def settle_fine(q):
        t, rows = BODY + q // 2, slice(q % 2 * FINE, q % 2 * FINE + FINE)
        c_fine(q).wait_recv()
        for u in range(2):
            src, zz, g, k = piece(t, u)
            half = q // 2
            if q % 2 == 0:
                near_copy(t, u, g, half, 0).wait_recv()
                near_copy(t, u, g, half, 1).wait_recv()
            value = part[t, u, core, rows, :] + c_in[t, u, rows, :]
            value = value + (near_in[g, u, half, 0, rows, :] + near_in[g, u, half, 1, rows, :])
            target = src * 2 + zz

            @pl.when(target != z)
            def _():
                s_out[t, u, rows, :] = value
                pltpu.make_async_remote_copy(
                    src_ref=s_out.at[t, u, pl.ds(q % 2 * FINE, FINE)],
                    dst_ref=z_in.at[
                        half, (z + NZ - target + NZ - 1) % NZ, pl.ds(q % 2 * FINE, FINE)
                    ],
                    send_sem=z_send,
                    recv_sem=z_recv.at[half],
                    device_id=(target * 2 + core, x, y),
                    device_id_type=MESH,
                ).start()

            @pl.when(target == z)
            def _():
                r_own[half, rows, :] = value

    for q in range(4):
        for side in range(2):
            rows = pl.ds(q % 2 * FINE, FINE)
            piece_half = a_all.at[BODY + q // 2, side, :, rows]
            pltpu.make_async_copy(piece_half, piece_half, fine_recv.at[side, q]).wait()
        compute_fine(q)
        if q > 0:
            settle_fine(q - 1)
    settle_fine(3)

    def all_of(ref, sem):
        pltpu.make_async_copy(ref, ref, sem).wait()

    all_of(a_all.at[pl.ds(NK, NJ)], a_send)
    all_of(c_in, c_send)
    all_of(far_in, far_send)
    all_of(near_in, near_send)
    all_of(z_in, z_send)
    for k in range(3):
        flag_send(t2_mask, x, k).wait_send()

    for half in range(NQ):
        all_of(z_in.at[half], z_recv.at[half])
        total = r_own[half]
        for k in range(NZ - 1):
            total = total + z_in[half, k]
        out[half * SUB : (half + 1) * SUB, :] = total


def per_device(residual, amplitudes, integrals, t2_mask, v_mask):
    f32, bf16, dma = jnp.float32, jnp.bfloat16, pltpu.SemaphoreType.DMA
    summed = pl.pallas_call(
        kernel,
        out_shape=jax.ShapeDtypeStruct((32, AB), f32),
        in_specs=[pl.BlockSpec(memory_space=pl.ANY)] * 4,
        out_specs=pl.BlockSpec(memory_space=pltpu.VMEM),
        scratch_shapes=[
            pltpu.VMEM((STEPS, 2, 2, SUB, CD), f32),
            pltpu.VMEM((CD, AB), f32),
            pltpu.VMEM((CD, AB), bf16),
            pltpu.VMEM((CD, AB), bf16),
            pltpu.VMEM((2 * ROWS, CD), bf16),
            pltpu.VMEM((STEPS, 2, 2, SUB, AB), f32),
            pltpu.VMEM((STEPS, 2, SUB, AB), f32),
            pltpu.VMEM((STEPS, 2, SUB, AB), f32),
            pltpu.VMEM((4, 2, NQ, 2, SUB, HALF), f32),
            pltpu.VMEM((4, 2, NQ, 2, SUB, AB), f32),
            pltpu.VMEM((NQ, SUB, AB), f32),
            pltpu.VMEM((NQ, NZ - 1, SUB, AB), f32),
            pltpu.VMEM((NX, 4, 8), jnp.int32),
            pltpu.VMEM((8, 8), jnp.int32),
            pltpu.VMEM((16, 1, CD), f32),
            dma(()),
            dma((2, NJ)),
            dma((2, NK)),
            dma((8,)),
            dma((3,)),
            dma((3,)),
            dma((2,)),
            dma(()),
            dma((STEPS,)),
            dma(()),
            dma((4, 4 * NQ)),
            dma(()),
            dma((4, 4 * NQ)),
            dma(()),
            dma((NQ,)),
            pltpu.SemaphoreType.REGULAR((3, 2)),
            dma((2, 4)),
            dma((4,)),
        ],
        compiler_params=pltpu.CompilerParams(
            collective_id=0, has_side_effects=True, vmem_limit_bytes=56 * 1024 * 1024
        ),
        name="ladder",
    )(amplitudes.reshape(2, 2, NY, NQ, SUB, CD), integrals, t2_mask, v_mask)
    return residual + summed


def solution(mesh):
    in_specs = (
        P(("row", "depth"), "col"),
        P("col", ("row", "depth")),
        P(("row", "depth"), "col"),
        P("col", ("row", "depth")),
        P(("row", "depth"), "col"),
    )
    out_specs = P(("row", "depth"), "col")
    return jax.shard_map(
        per_device, mesh=mesh, in_specs=in_specs, out_specs=out_specs, check_vma=False
    )
```

```python
import jax
import jax.numpy as jnp
from jax import lax
from jax.experimental import pallas as pl
from jax.experimental.pallas import tpu as pltpu
from jax.sharding import PartitionSpec as P

TILE = 128
NX, NY, NZ = 4, 4, 8
SUB = 16
NQ = 32 // SUB
NK = NY * NQ
NJ = 3 * NK
STEPS = NK + NJ
CD = 1024
AB = 1024
HALF = AB // 2
ROWS = 4 * SUB
MESH = pl.DeviceIdType.MESH
LAG = 1
LATE = 28
BODY = STEPS - 2
FINE = SUB // 2


def expand_lanes(flags):
    values = flags.astype(jnp.float32)
    return jnp.concatenate(
        [jnp.broadcast_to(values[:, q : q + 1], (values.shape[0], TILE)) for q in range(8)],
        axis=1,
    )


def kernel(
    amp, integ, t2_mask, v_mask, out,
    a_all, v_f32, v_hi, v_lo, a_hl, part, c_in, s_out, far_in, near_in,
    r_own, z_in, t2_all, v_flags, a_flags,
    a_send, a_recv, own_sem, v_sem, m_send, m_recv, m_sem, c_send, c_recv,
    far_send, far_recv, near_send, near_recv, z_send, z_recv, z_known, fine_recv, c_fine_recv,
):
    row = lax.axis_index("row")
    x = lax.axis_index("col")
    y = lax.axis_index("depth")
    z = row // 2
    core = row % 2
    right, left = (x + 1) % NX, (x + 3) % NX
    up, down = (y + 1) % NY, (y + 3) % NY
    sibling = z * 2 + 1 - core
    z_next = ((z + 1) % NZ) * 2 + core
    z_prev = ((z + NZ - 1) % NZ) * 2 + core

    barrier = pltpu.get_barrier_semaphore()

    def greet(r, c, d):
        pl.semaphore_signal(barrier, inc=1, device_id=(r, c, d), device_id_type=MESH)

    greet(row, left, y)
    greet(row, right, y)
    greet(sibling, x, y)
    greet(row, x, up)
    greet(row, x, down)
    greet(z_next, x, y)
    greet(z_prev, x, y)

    def rows_of(k, side):
        middle = (k >= NQ) & (k < 3 * NQ)
        turn = (k + NQ + side) % 2
        kind = jnp.where(k < NQ, 0, jnp.where(middle, 1 + turn, 3))
        owner = (y + jnp.where(k < NQ, 2, jnp.where(middle, 1 + 2 * turn, 0))) % NY
        part_of = jnp.where(middle, (k + NQ) // 2 % NQ, k % NQ)
        return kind, owner, part_of

    block = z // 2
    turn_in = (x + NX - 1 - block) % NX, (x + 1 + NX - block) % NX
    turn_out = (x + NX - block) % NX
    f_last = (
        (turn_in[0] == 1) | (turn_in[0] == 2),
        (turn_in[1] == 3) | (turn_in[1] == 2),
    )
    f_last_out = (turn_out == 1) | (turn_out == 2), (turn_out == 3) | (turn_out == 2)

    def b_slot(k, side):
        late = 0 if k < NK // 2 else jnp.where(f_last_out[side], 0, NK)
        return NK + k + late

    def f_slot(k, side):
        return k + jnp.where(f_last_out[side], 2 * NK, NK + NK // 2)

    def piece(t, side):
        j = t - NK
        split_b = jnp.where(j < NK + NK // 2, 2, jnp.where(j < 2 * NK + NK // 2, 3, 2))
        split_k = jnp.where(
            j < NK + NK // 2, j - NK, jnp.where(j < 2 * NK + NK // 2, j - NK - NK // 2, j - 2 * NK)
        )
        whole_b = jnp.where(j < 2 * NK, 2, 3)
        whole_k = jnp.where(j < 2 * NK, j - NK, j - 2 * NK)
        later_g = jnp.where(f_last[side], whole_b, split_b)
        later_k = jnp.where(f_last[side], whole_k, split_k)
        g = jnp.where(t < NK, 0, jnp.where(j < NK, 1, later_g))
        k = jnp.where(t < NK, t, jnp.where(j < NK, j, later_k))
        away = jnp.where(g == 0, 0, jnp.where(g == 3, 2, 1))
        zz = jnp.where(g == 2, 1 - side, side)
        src = (x + NX - away) % NX if side == 0 else (x + away) % NX
        return src, zz, g, k

    def own_copy(k, zz):
        _, owner, half = rows_of(k, zz)
        return pltpu.make_async_copy(
            amp.at[zz, :, owner, half], a_all.at[k, zz], own_sem.at[zz, k]
        )

    def v_copy(q):
        at = pl.ds(q * TILE, TILE)
        return pltpu.make_async_copy(integ.at[at, :], v_f32.at[at, :], v_sem.at[q])

    m_copy = pltpu.make_async_copy(t2_mask, t2_all.at[x], m_sem.at[0])
    vm_copy = pltpu.make_async_copy(v_mask, v_flags, m_sem.at[1])
    vm_copy.start()
    for q in range(8):
        v_copy(q).start()
    m_copy.start()
    pl.semaphore_wait(barrier, 7)

    def a_own_send(slot, zz, k, side):
        _, owner, half = rows_of(k, side)
        return pltpu.make_async_remote_copy(
            src_ref=amp.at[zz, :, owner, half],
            dst_ref=a_all.at[NK + slot, side],
            send_sem=a_send,
            recv_sem=a_recv.at[side, slot],
            device_id=(row, right if side == 0 else left, y),
            device_id_type=MESH,
        )

    def a_own_fine(zz, k, side, e):
        _, owner, half = rows_of(k, side)
        rows = pl.ds(e * FINE, FINE)
        return pltpu.make_async_remote_copy(
            src_ref=amp.at[zz, :, owner, half, rows],
            dst_ref=a_all.at[STEPS - NK + k, side, :, rows],
            send_sem=a_send,
            recv_sem=fine_recv.at[side, (k - NK + 2) * 2 + e],
            device_id=(row, right if side == 0 else left, y),
            device_id_type=MESH,
        )

    def a_forward_fine(k, side, e):
        rows = pl.ds(e * FINE, FINE)
        return pltpu.make_async_remote_copy(
            src_ref=a_all.at[NK + k, side, :, rows],
            dst_ref=a_all.at[STEPS - NK + k, side, :, rows],
            send_sem=a_send,
            recv_sem=fine_recv.at[side, (k - NK + 2) * 2 + e],
            device_id=(row, right if side == 0 else left, y),
            device_id_type=MESH,
        )

    def a_forward(k, side):
        slot = f_slot(k, side)
        return pltpu.make_async_remote_copy(
            src_ref=a_all.at[NK + k, side],
            dst_ref=a_all.at[NK + slot, side],
            send_sem=a_send,
            recv_sem=a_recv.at[side, slot],
            device_id=(row, right if side == 0 else left, y),
            device_id_type=MESH,
        )

    def flag_send(src, who, k):
        return pltpu.make_async_remote_copy(
            src_ref=src,
            dst_ref=t2_all.at[who],
            send_sem=m_send.at[k],
            recv_sem=m_recv.at[k],
            device_id=(row, left if k == 1 else right, y),
            device_id_type=MESH,
        )

    for k in range(NK):
        for side in range(2):
            a_own_send(k, side, k, side).start()
    flag_send(t2_mask, x, 0).start()
    flag_send(t2_mask, x, 1).start()
    for k in range(NK):
        own_copy(k, 0).start()
        own_copy(k, 1).start()
    for k in range(NK // 2):
        for side in range(2):
            a_own_send(b_slot(k, side), 1 - side, k, side).start()
    for side in range(2):
        @pl.when(f_last_out[side])
        def _():
            for k in range(NK // 2, NK):
                a_own_send(b_slot(k, side), 1 - side, k, side).start()

    vm_copy.wait()
    flags_v = expand_lanes(v_flags[...])
    for q in range(8):
        v_copy(q).wait()
        rows = slice(q * TILE, (q + 1) * TILE)
        kept = v_f32[rows, :] * flags_v[q : q + 1, :]
        hi = kept.astype(jnp.bfloat16)
        v_hi[rows, :] = hi
        v_lo[rows, :] = (kept - hi.astype(jnp.float32)).astype(jnp.bfloat16)

    def widen(s):
        wide = expand_lanes(t2_all[s])
        for p in range(4):
            a_flags[s * 4 + p] = wide[p : p + 1, :]

    m_copy.wait()
    widen(x)

    def c_copy(t):
        return pltpu.make_async_remote_copy(
            src_ref=part.at[t, :, 1 - core],
            dst_ref=c_in.at[t],
            send_sem=c_send,
            recv_sem=c_recv.at[t],
            device_id=(sibling, x, y),
            device_id_type=MESH,
        )

    def far_copy(t, u, g, half, way):
        return pltpu.make_async_remote_copy(
            src_ref=s_out.at[t, u, :, pl.ds(way * HALF, HALF)],
            dst_ref=far_in.at[g, u, half, way],
            send_sem=far_send,
            recv_sem=far_recv.at[g, u * 2 * NQ + half * 2 + way],
            device_id=(row, x, up if way == 0 else down),
            device_id_type=MESH,
        )

    def near_copy(t, u, g, half, way):
        return pltpu.make_async_remote_copy(
            src_ref=s_out.at[t, u],
            dst_ref=near_in.at[g, u, half, way],
            send_sem=near_send,
            recv_sem=near_recv.at[g, u * 2 * NQ + half * 2 + way],
            device_id=(row, x, up if way == 0 else down),
            device_id_type=MESH,
        )

    def z_copy(t, u, half, target):
        return pltpu.make_async_remote_copy(
            src_ref=s_out.at[t, u],
            dst_ref=z_in.at[half, (z + NZ - target + NZ - 1) % NZ],
            send_sem=z_send,
            recv_sem=z_recv.at[half],
            device_id=(target * 2 + core, x, y),
            device_id_type=MESH,
        )

    def settle(t):
        c_copy(t).wait_recv()
        for u in range(2):
            src, zz, g, k = piece(t, u)
            kind, _, half = rows_of(k, u)

            @pl.when(kind == 0)
            def _():
                s_out[t, u] = part[t, u, core] + c_in[t, u]
                far_copy(t, u, g, half, 0).start()
                far_copy(t, u, g, half, 1).start()

            for way in range(2):
                @pl.when(kind == 1 + way)
                def _():
                    far_copy(t, u, g, half, way).wait_recv()
                    for w in range(2):
                        lanes = slice(w * HALF, (w + 1) * HALF)
                        value = part[t, u, core, :, lanes] + c_in[t, u, :, lanes]
                        if w == way:
                            value = value + far_in[g, u, half, way]
                        s_out[t, u, :, lanes] = value
                    near_copy(t, u, g, half, way).start()

            @pl.when(kind == 3)
            def _():
                near_copy(t, u, g, half, 0).wait_recv()
                near_copy(t, u, g, half, 1).wait_recv()
                value = part[t, u, core] + c_in[t, u]
                value = value + (near_in[g, u, half, 0] + near_in[g, u, half, 1])
                target = src * 2 + zz

                @pl.when(target != z)
                def _():
                    s_out[t, u] = value
                    z_copy(t, u, half, target).start()

                @pl.when(target == z)
                def _():
                    r_own[half] = value

    def compute(t):
        for side in range(2):
            src, zz, _, _ = piece(t, side)
            for c in range(2):
                kept = a_all[t, side, c] * a_flags[src * 4 + zz * 2 + c]
                hi = kept.astype(jnp.bfloat16)
                lo = (kept - hi.astype(jnp.float32)).astype(jnp.bfloat16)
                at = (side * 2 + c) * SUB
                a_hl[at : at + SUB, :] = hi
                a_hl[at + ROWS : at + ROWS + SUB, :] = lo
        for m in range(AB // 256):
            lanes = slice(m * 256, m * 256 + 256)
            both = jnp.dot(a_hl[...], v_hi[:, lanes], preferred_element_type=jnp.float32)
            low = jnp.dot(a_hl[0:ROWS, :], v_lo[:, lanes], preferred_element_type=jnp.float32)
            total = both[0:ROWS, :] + (both[ROWS:, :] + low)
            part[t, :, :, :, lanes] = total.reshape(2, 2, SUB, 256)
        c_copy(t).start()

    def know(r):
        for way, who in ((0, z_next), (1, z_prev)):
            pl.semaphore_signal(
                z_known.at[r, way], inc=1, device_id=(who, x, y), device_id_type=MESH
            )

    def known(r):
        pl.semaphore_wait(z_known.at[r, 0], 1)
        pl.semaphore_wait(z_known.at[r, 1], 1)

    @pl.loop(0, BODY)
    def _(t):
        for r in range(3):
            @pl.when(t == 2 * r)
            def _():
                if r > 0:
                    known(r - 1)
                know(r)

        @pl.when(t == NK - 2)
        def _():
            known(2)

        @pl.when(t >= LATE)
        def _():
            settle(t - LAG)

        @pl.when(t < NK)
        def _():
            own_copy(t, 0).wait()
            own_copy(t, 1).wait()

        @pl.when(t == NK)
        def _():
            flag_send(t2_mask, x, 0).wait_recv()
            flag_send(t2_mask, x, 1).wait_recv()
            flag_send(t2_all.at[left], left, 2).start()
            widen(left)
            widen(right)

        @pl.when(t == 2 * NK + NK // 2)
        def _():
            flag_send(t2_all.at[left], left, 2).wait_recv()
            widen((x + 2) % NX)

        @pl.when(t >= NK)
        def _():
            for side in range(2):
                pltpu.make_async_copy(
                    a_all.at[t, side], a_all.at[t, side], a_recv.at[side, t - NK]
                ).wait()

        @pl.when((t >= NK) & (t < 2 * NK))
        def _():
            for side in range(2):
                fine = f_last_out[side] & (t >= 2 * NK - 2)

                @pl.when(jnp.logical_not(fine))
                def _():
                    a_forward(t - NK, side).start()

                @pl.when(fine)
                def _():
                    for e in range(2):
                        a_forward_fine(t - NK, side, e).start()

        for side in range(2):
            @pl.when((t == 2 * NK - 1) & jnp.logical_not(f_last_out[side]))
            def _():
                for k in range(NK // 2, NK - 2):
                    a_own_send(b_slot(k, side), 1 - side, k, side).start()
                for k in range(NK - 2, NK):
                    for e in range(2):
                        a_own_fine(1 - side, k, side, e).start()

        compute(t)

        @pl.when((t >= LAG) & (t < LATE))
        def _():
            settle(t - LAG)

    settle(BODY - 1)

    def c_fine(q):
        rows = pl.ds(q % 2 * FINE, FINE)
        return pltpu.make_async_remote_copy(
            src_ref=part.at[BODY + q // 2, :, 1 - core, rows],
            dst_ref=c_in.at[BODY + q // 2, :, rows],
            send_sem=c_send,
            recv_sem=c_fine_recv.at[q],
            device_id=(sibling, x, y),
            device_id_type=MESH,
        )

    def compute_fine(q):
        t, rows = BODY + q // 2, slice(q % 2 * FINE, q % 2 * FINE + FINE)
        kept = []
        for side in range(2):
            src, zz, _, _ = piece(t, side)
            for c in range(2):
                kept.append(a_all[t, side, c, rows, :] * a_flags[src * 4 + zz * 2 + c])
        kept = jnp.concatenate(kept, axis=0)
        hi = kept.astype(jnp.bfloat16)
        lo = (kept - hi.astype(jnp.float32)).astype(jnp.bfloat16)
        n = 4 * FINE
        a_hl[0:n, :] = hi
        a_hl[n : 2 * n, :] = lo
        for m in range(AB // 256):
            lanes = slice(m * 256, m * 256 + 256)
            both = jnp.dot(a_hl[0 : 2 * n, :], v_hi[:, lanes], preferred_element_type=jnp.float32)
            low = jnp.dot(a_hl[0:n, :], v_lo[:, lanes], preferred_element_type=jnp.float32)
            total = both[0:n, :] + (both[n:, :] + low)
            part[t, :, :, rows, lanes] = total.reshape(2, 2, FINE, 256)
        c_fine(q).start()

    def settle_fine(q):
        t, rows = BODY + q // 2, slice(q % 2 * FINE, q % 2 * FINE + FINE)
        c_fine(q).wait_recv()
        for u in range(2):
            src, zz, g, k = piece(t, u)
            half = q // 2
            if q % 2 == 0:
                near_copy(t, u, g, half, 0).wait_recv()
                near_copy(t, u, g, half, 1).wait_recv()
            value = part[t, u, core, rows, :] + c_in[t, u, rows, :]
            value = value + (near_in[g, u, half, 0, rows, :] + near_in[g, u, half, 1, rows, :])
            target = src * 2 + zz

            @pl.when(target != z)
            def _():
                s_out[t, u, rows, :] = value
                pltpu.make_async_remote_copy(
                    src_ref=s_out.at[t, u, pl.ds(q % 2 * FINE, FINE)],
                    dst_ref=z_in.at[
                        half, (z + NZ - target + NZ - 1) % NZ, pl.ds(q % 2 * FINE, FINE)
                    ],
                    send_sem=z_send,
                    recv_sem=z_recv.at[half],
                    device_id=(target * 2 + core, x, y),
                    device_id_type=MESH,
                ).start()

            @pl.when(target == z)
            def _():
                r_own[half, rows, :] = value

    for q in range(4):
        for side in range(2):
            rows = pl.ds(q % 2 * FINE, FINE)
            piece_half = a_all.at[BODY + q // 2, side, :, rows]
            pltpu.make_async_copy(piece_half, piece_half, fine_recv.at[side, q]).wait()
        compute_fine(q)
        if q > 0:
            settle_fine(q - 1)
    settle_fine(3)

    def all_of(ref, sem):
        pltpu.make_async_copy(ref, ref, sem).wait()

    for half in range(NQ):
        all_of(z_in.at[half], z_recv.at[half])
        total = r_own[half]
        for k in range(NZ - 1):
            total = total + z_in[half, k]
        out[half * SUB : (half + 1) * SUB, :] = total

    all_of(a_all.at[pl.ds(NK, NJ)], a_send)
    all_of(c_in, c_send)
    all_of(far_in, far_send)
    all_of(near_in, near_send)
    all_of(z_in, z_send)
    for k in range(3):
        flag_send(t2_mask, x, k).wait_send()


def per_device(residual, amplitudes, integrals, t2_mask, v_mask):
    f32, bf16, dma = jnp.float32, jnp.bfloat16, pltpu.SemaphoreType.DMA
    summed = pl.pallas_call(
        kernel,
        out_shape=jax.ShapeDtypeStruct((32, AB), f32),
        in_specs=[pl.BlockSpec(memory_space=pl.ANY)] * 4,
        out_specs=pl.BlockSpec(memory_space=pltpu.VMEM),
        scratch_shapes=[
            pltpu.VMEM((STEPS, 2, 2, SUB, CD), f32),
            pltpu.VMEM((CD, AB), f32),
            pltpu.VMEM((CD, AB), bf16),
            pltpu.VMEM((CD, AB), bf16),
            pltpu.VMEM((2 * ROWS, CD), bf16),
            pltpu.VMEM((STEPS, 2, 2, SUB, AB), f32),
            pltpu.VMEM((STEPS, 2, SUB, AB), f32),
            pltpu.VMEM((STEPS, 2, SUB, AB), f32),
            pltpu.VMEM((4, 2, NQ, 2, SUB, HALF), f32),
            pltpu.VMEM((4, 2, NQ, 2, SUB, AB), f32),
            pltpu.VMEM((NQ, SUB, AB), f32),
            pltpu.VMEM((NQ, NZ - 1, SUB, AB), f32),
            pltpu.VMEM((NX, 4, 8), jnp.int32),
            pltpu.VMEM((8, 8), jnp.int32),
            pltpu.VMEM((16, 1, CD), f32),
            dma(()),
            dma((2, NJ)),
            dma((2, NK)),
            dma((8,)),
            dma((3,)),
            dma((3,)),
            dma((2,)),
            dma(()),
            dma((STEPS,)),
            dma(()),
            dma((4, 4 * NQ)),
            dma(()),
            dma((4, 4 * NQ)),
            dma(()),
            dma((NQ,)),
            pltpu.SemaphoreType.REGULAR((3, 2)),
            dma((2, 4)),
            dma((4,)),
        ],
        compiler_params=pltpu.CompilerParams(
            collective_id=0, has_side_effects=True, vmem_limit_bytes=56 * 1024 * 1024
        ),
        name="ladder",
    )(amplitudes.reshape(2, 2, NY, NQ, SUB, CD), integrals, t2_mask, v_mask)
    return residual + summed


def solution(mesh):
    in_specs = (
        P(("row", "depth"), "col"),
        P("col", ("row", "depth")),
        P(("row", "depth"), "col"),
        P("col", ("row", "depth")),
        P(("row", "depth"), "col"),
    )
    out_specs = P(("row", "depth"), "col")
    return jax.shard_map(
        per_device, mesh=mesh, in_specs=in_specs, out_specs=out_specs, check_vma=False
    )
```
